256 devices in a mesh: expert: 64 (over y, z, core), dp: 4 (over x).
Axes of the slice: x: 4, y: 4, z: 8, core: 2. Of those that a mesh axis runs over, the one named last changes fastest.
Arguments:
- tokens: bfloat16 [32768, 1440], P(('expert', 'dp')), may hold values from -6 to 6
- routes: int32 [32768, 4], P(('expert', 'dp')), may hold values from 0 to 63, as said below
- gate_fixed: int32 [32768, 4], P(('expert', 'dp')), may hold values from 4096 to 65535
- counts: int32 [256], P(('expert', 'dp')), may hold values from 32 to 128, as said below
- replica_plan: int32 [8], replicated, may hold values from 0 to 63, as said below
- weight_in: bfloat16 [64, 1440, 1440], P('expert', None, 'dp'), may hold values from -0.15625 to 0.15625
- weight_out: bfloat16 [64, 1440, 1440], P('expert', 'dp'), may hold values from -0.15625 to 0.15625
- cotangent: bfloat16 [32768, 1440], P(('expert', 'dp')), may hold values from -0.59765625 to 0.59765625
Outputs:
- layer_output: bfloat16 [32768, 1440], P(('expert', 'dp'))
- input_grads: bfloat16 [32768, 1440], P(('expert', 'dp'))
- weight_in_grad: bfloat16 [64, 1440, 1440], P('expert', None, 'dp')
- weight_out_grad: bfloat16 [64, 1440, 1440], P('expert', 'dp')
The draws below stay inside these ranges and needn't reach their ends.
Inputs may be any that keep to these rules, and one draw needn't show every extreme that they name: `routes`: each row names 4 different experts. `replica_plan`: 8 different experts, among them 0, 31, 32 and 63, in any order. `counts`: some device has 128 live tokens in every draw.
All inputs are finite; a program needn't handle non-finite values.
Results may differ from the reference program's by a relative error of at most 0.0064.
Values may be sent and summed in bfloat16 or wider, within the bound.
No kernel may reach another device: no remote copies, remote signals or barrier semaphores. Data moves between devices by JAX's collectives and lax.ppermute only.
A program may use at most 128 MiB of HBM per device.

```python
import jax
import jax.numpy as jnp
from jax import lax

D = 1440
FF = 1440
PATHS_EACH_WORD = 4
TOK_DEV = 128
SPECIALIST_NUM = 64
WORD_SUM = 32768
HOT = 8
CAP = 3
SPARE = 1
DEVICES = 256


def hot_experts(key):
    half_experts = SPECIALIST_NUM // 2
    expert_ids = jnp.arange(SPECIALIST_NUM, dtype=jnp.int32)
    pinned = ((expert_ids == 0) | (expert_ids == half_experts - 1) | (expert_ids == half_experts) | (expert_ids == SPECIALIST_NUM - 1)).astype(jnp.int32)
    priority = jax.random.permutation(jax.random.fold_in(key, 71), SPECIALIST_NUM).astype(jnp.int32)
    scores = priority + pinned * SPECIALIST_NUM
    chosen_scores, chosen = lax.top_k(scores, HOT)
    order = jax.random.permutation(jax.random.fold_in(key, 72), HOT).astype(jnp.int32)
    return chosen.astype(jnp.int32)[order].astype(jnp.int32)


def draw_replica_plan(key, part):
    return hot_experts(key)


def draw_routes(key, part):
    hot_list = hot_experts(key)
    frequent_indicator = jnp.sum((hot_list[:, None] == jnp.arange(SPECIALIST_NUM, dtype=jnp.int32)[None, :]).astype(jnp.int32), axis=0)
    unboosted_logit = jax.random.randint(jax.random.fold_in(key, 73), (WORD_SUM, SPECIALIST_NUM), 0, 1024, dtype=jnp.int32)
    frequent_uplift = (jax.random.randint(jax.random.fold_in(key, 74), (WORD_SUM, SPECIALIST_NUM), 0, SPECIALIST_NUM, dtype=jnp.int32) < 2 * PATHS_EACH_WORD).astype(jnp.int32) * frequent_indicator[None, :]
    specialist_logits = (unboosted_logit + 1024 * frequent_uplift) * SPECIALIST_NUM + jnp.arange(SPECIALIST_NUM, dtype=jnp.int32)[None, :]
    chosen_values, chosen = lax.top_k(specialist_logits, PATHS_EACH_WORD)
    return chosen.astype(jnp.int32)


def draw_counts(key, part):
    values = jax.random.randint(key, (DEVICES,), TOK_DEV // 4, TOK_DEV + 1, dtype=jnp.int32)
    chosen = jax.random.randint(jax.random.fold_in(key, 11), (), 0, DEVICES, dtype=jnp.int32)
    return jnp.where(jnp.arange(DEVICES, dtype=jnp.int32) == chosen, TOK_DEV, values).astype(jnp.int32)


def with_ends(drawn, own_key, low, high):
    extent = drawn.shape
    spot = [jax.random.randint(jax.random.fold_in(own_key, axis), (), 0, extent[axis]) for axis in range(len(extent))]
    drawn = drawn.at[tuple(spot)].set(low)
    longest = extent.index(max(extent))
    spot[longest] = (spot[longest] + 1) % extent[longest]
    return drawn.at[tuple(spot)].set(high)


def level_of(stream_key, shape, pieces, least, largest):
    loudness, own = 1.0, jax.random.fold_in(stream_key, 6)
    for dim, blocks in pieces:
        steps = jnp.exp(jax.random.uniform(jax.random.fold_in(own, dim), (blocks,), jnp.float32, least / len(pieces), largest / len(pieces)))
        loudness = loudness * jnp.repeat(steps, shape[dim] // blocks).reshape([-1 if axis == dim else 1 for axis in range(len(shape))])
    return loudness


def noise(key, extent, deviation, most, pieces=(), kind=jnp.bfloat16):
    result = deviation * jax.random.normal(key, extent, jnp.float32)
    if pieces:
        result = result * level_of(key, extent, pieces, -0.22, 0.18)
    return jnp.clip(result, -most, most).astype(kind)


def setup_inputs(seed: int = 0) -> dict:
    arg_keys = jax.random.split(jax.random.key(seed), 9)
    return {
        "tokens": noise(arg_keys[0], (WORD_SUM, D), 1.0, 6.0, ((0, 256),)),
        "routes": draw_routes(jax.random.fold_in(arg_keys[8], 71), 0),
        "gate_fixed": with_ends(jax.random.randint(arg_keys[2], (WORD_SUM, PATHS_EACH_WORD), 4096, 65536), jax.random.fold_in(arg_keys[2], 1), 4096, 65535).astype(jnp.int32),
        "counts": draw_counts(jax.random.fold_in(arg_keys[8], 71), 0),
        "replica_plan": draw_replica_plan(jax.random.fold_in(arg_keys[8], 71), 0),
        "weight_in": noise(arg_keys[5], (SPECIALIST_NUM, D, FF), D ** -0.5, 0.15625, ((0, 64), (2, 4))),
        "weight_out": noise(arg_keys[6], (SPECIALIST_NUM, FF, D), FF ** -0.5, 0.15625, ((0, 64), (1, 4))),
        "cotangent": noise(arg_keys[7], (WORD_SUM, D), 0.1, 0.59765625, ((0, 256),)),
    }


def activate(values):
    return values * jax.nn.sigmoid(1.702 * values)


def derivative(values):
    sigmoid_value = jax.nn.sigmoid(1.702 * values)
    return sigmoid_value + 1.702 * values * sigmoid_value * (1.0 - sigmoid_value)


def slot_tables(routes, live_count, frequent_indicator, experts, capacity, spare_slots):
    token_count, top_count = routes.shape
    slot_width = capacity + spare_slots
    active = (jnp.arange(token_count, dtype=jnp.int32) < live_count).astype(jnp.int32)
    flattened = routes.reshape(-1).astype(jnp.int32)
    active_flat = jnp.repeat(active, top_count, total_repeat_length=token_count * top_count)
    same_expert = (flattened[:, None] == jnp.arange(experts, dtype=jnp.int32)[None, :]).astype(jnp.int32)
    matches = same_expert * active_flat[:, None]
    before = jnp.cumsum(matches, axis=0) - matches
    position = jnp.sum(before * matches, axis=1).astype(jnp.int32)
    hot_route = jnp.sum(same_expert * frequent_indicator[None, :], axis=1).astype(jnp.int32)
    keep_route = (active_flat > 0) & (position < capacity + spare_slots * hot_route)
    target_block = jnp.where(position < capacity, flattened, (flattened + experts // 2) % experts).astype(jnp.int32)
    slot_index = jnp.where(keep_route, target_block * slot_width + position, experts * slot_width).astype(jnp.int32)
    source = jnp.full((experts * slot_width + 1,), -1, jnp.int32)
    source = source.at[slot_index].set(jnp.arange(token_count * top_count, dtype=jnp.int32))
    return slot_index, source[:experts * slot_width]


def reference(tokens, routes, gate_fixed, counts, replica_plan, weight_in, weight_out, cotangent):
    devices = counts.shape[0]
    slot_width = CAP + SPARE
    frequent_indicator = jnp.sum((replica_plan[:, None] == jnp.arange(SPECIALIST_NUM, dtype=jnp.int32)[None, :]).astype(jnp.int32), axis=0).astype(jnp.int32)
    per_device = routes.reshape(devices, TOK_DEV, PATHS_EACH_WORD)
    slot_all, source_all = jax.vmap(lambda block_routes, live_count: slot_tables(block_routes, live_count, frequent_indicator, SPECIALIST_NUM, CAP, SPARE))(per_device, counts)
    offsets = (jnp.arange(devices, dtype=jnp.int32) * (TOK_DEV * PATHS_EACH_WORD))[:, None]
    global_ids = jnp.where(source_all >= 0, source_all + offsets, -1).astype(jnp.int32).reshape(devices, SPECIALIST_NUM, slot_width)
    partner = ((jnp.arange(SPECIALIST_NUM, dtype=jnp.int32) + SPECIALIST_NUM // 2) % SPECIALIST_NUM).astype(jnp.int32)
    expert_ids = jnp.concatenate([global_ids[:, :, :CAP], global_ids[:, partner, CAP:]], axis=2)
    expert_ids = expert_ids.transpose(1, 0, 2).reshape(SPECIALIST_NUM, devices * slot_width)
    scales = gate_fixed.reshape(-1).astype(jnp.float32) / 65536.0

    def per_expert(expert):
        route_ids = expert_ids[expert]
        filled = (route_ids >= 0)[:, None]
        clipped = jnp.maximum(route_ids, 0).astype(jnp.int32)
        token_ids = (clipped // PATHS_EACH_WORD).astype(jnp.int32)
        inputs = jnp.where(filled, tokens[token_ids], jnp.zeros((), tokens.dtype))
        grad_rows = jnp.where(filled, scales[clipped][:, None] * cotangent[token_ids].astype(jnp.float32), 0.0).astype(jnp.bfloat16)
        w_first = weight_in[expert]
        w_second = weight_out[expert]
        preact = jnp.dot(inputs, w_first, preferred_element_type=jnp.float32)
        activation = activate(preact).astype(jnp.bfloat16)
        outputs = jnp.dot(activation, w_second, preferred_element_type=jnp.float32).astype(jnp.bfloat16)
        act_grad = jnp.dot(grad_rows, w_second.T, preferred_element_type=jnp.float32)
        pre_grad = (act_grad * derivative(preact)).astype(jnp.bfloat16)
        input_rows = jnp.dot(pre_grad, w_first.T, preferred_element_type=jnp.float32).astype(jnp.bfloat16)
        grad_first = jnp.dot(inputs.T, pre_grad, preferred_element_type=jnp.float32).astype(jnp.bfloat16)
        grad_second = jnp.dot(activation.T, grad_rows, preferred_element_type=jnp.float32).astype(jnp.bfloat16)
        return outputs, input_rows, grad_first, grad_second

    outputs, input_rows, grad_first, grad_second = lax.map(per_expert, jnp.arange(SPECIALIST_NUM, dtype=jnp.int32))
    targets = jnp.where(expert_ids >= 0, expert_ids, WORD_SUM * PATHS_EACH_WORD).astype(jnp.int32).reshape(-1)
    route_out = jnp.zeros((WORD_SUM * PATHS_EACH_WORD + 1, D), outputs.dtype).at[targets].set(outputs.reshape(-1, D))[:-1]
    route_dx = jnp.zeros((WORD_SUM * PATHS_EACH_WORD + 1, D), input_rows.dtype).at[targets].set(input_rows.reshape(-1, D))[:-1]
    weighted = route_out.astype(jnp.float32) * scales[:, None]
    layer_output = jnp.sum(weighted.reshape(WORD_SUM, PATHS_EACH_WORD, D), axis=1).astype(jnp.bfloat16)
    input_grads = jnp.sum(route_dx.astype(jnp.float32).reshape(WORD_SUM, PATHS_EACH_WORD, D), axis=1).astype(jnp.bfloat16)
    return layer_output, input_grads, grad_first, grad_second
```

```python
import jax
import jax.numpy as jnp
from jax import lax
from jax.sharding import PartitionSpec as P


def moved(value, steps):
    count = lax.axis_size("dp")
    return lax.ppermute(value, "dp", [(s, (s + steps) % count) for s in range(count)])


def ring(value, cut):
    top, bottom = value[:cut], value[cut:]
    left_top = moved(top, 1)
    right_bottom = moved(bottom, -1)
    left_bottom = moved(bottom, 1)
    right_top = moved(top, -1)
    far_top = moved(left_top, 1)
    far_bottom = moved(right_bottom, -1)
    return [(top, bottom), (left_top, left_bottom), (right_top, right_bottom), (far_top, far_bottom)]


def dot(a, b, ca, cb):
    return lax.dot_general(a, b, (((ca,), (cb,)), ((), ())), preferred_element_type=jnp.float32)


def both(pre):
    s = jax.nn.sigmoid(1.702 * pre)
    return pre * s, s + 1.702 * pre * s * (1.0 - s)


def tables(routes, gates, live_count, plan, experts, capacity, spare):
    token_count, top_count = routes.shape
    width = capacity + spare
    routes_t = routes.T
    gates_t = gates.T.astype(jnp.float32)
    ids = lax.broadcasted_iota(jnp.int32, (experts, token_count), 0)
    times = lax.broadcasted_iota(jnp.int32, (experts, token_count), 1)
    hits = jnp.zeros((experts, token_count), jnp.float32)
    gate = jnp.zeros((experts, token_count), jnp.float32)
    for k in range(top_count):
        same = routes_t[k][None, :] == ids
        hits = hits + jnp.where(same, 1.0, 0.0)
        gate = gate + jnp.where(same, gates_t[k][None, :], 0.0)
    hits = jnp.where(times < live_count, hits, 0.0)
    earlier = (
        lax.broadcasted_iota(jnp.int32, (token_count, token_count), 0)
        < lax.broadcasted_iota(jnp.int32, (token_count, token_count), 1)
    )
    before = dot(hits.astype(jnp.bfloat16), earlier.astype(jnp.bfloat16), 1, 0)
    hot = jnp.sum(
        (plan[None, :] == jnp.arange(experts, dtype=jnp.int32)[:, None]).astype(jnp.float32), axis=1
    )
    limit = capacity + spare * hot
    row = lax.broadcasted_iota(jnp.int32, (experts, 2 * width, token_count), 1)
    slot = (row % width).astype(jnp.float32)
    keep = (
        (hits[:, None, :] > 0.0)
        & (before[:, None, :] == slot)
        & (slot < limit[:, None, None])
    )
    first = row < width
    one = jnp.where(keep, 1.0, 0.0)
    level = jnp.where(keep, gate[:, None, :], 0.0)
    high = jnp.floor(level * (1.0 / 256.0))
    low = level - 256.0 * high
    high = high * (1.0 / 256.0)
    low = low * (1.0 / 65536.0)
    rows = experts * 2 * width

    def flat(part):
        return part.reshape(rows, token_count).astype(jnp.bfloat16)

    sending = jnp.concatenate(
        [
            flat(jnp.where(first, one, 0.0)),
            flat(jnp.where(first, 0.0, high)),
            flat(jnp.where(first, 0.0, low)),
        ],
        axis=1,
    )
    getting = jnp.concatenate(
        [
            flat(jnp.where(first, high, 0.0)),
            flat(jnp.where(first, low, 0.0)),
            flat(jnp.where(first, 0.0, one)),
        ],
        axis=1,
    )
    return sending, getting


def on_device(tokens, routes, gate_fixed, counts, replica_plan, weight_in, weight_out, cotangent):
    token_count, features = tokens.shape
    top_count = routes.shape[1]
    groups = lax.axis_size("expert")
    experts = groups * weight_in.shape[0]
    capacity = 3 * token_count * top_count // (8 * experts)
    spare = capacity // 2
    width = capacity + spare
    w_in = weight_in[0]
    w_out = weight_out[0]
    hidden = w_out.shape[0]
    ins = ring(w_in, features // 2)
    outs = ring(w_out, hidden // 16 * 8)
    sending, getting = tables(
        routes, gate_fixed, counts[0], replica_plan, experts, capacity, spare
    )
    source = jnp.concatenate([tokens, cotangent, cotangent], axis=0)
    rows = dot(sending, source, 1, 0).astype(jnp.bfloat16).reshape(experts, 2 * width, features)
    inbound = lax.all_to_all(rows, "expert", split_axis=0, concat_axis=0, tiled=True)
    blocks = [jnp.concatenate(b, axis=0) for b in ring(inbound, experts // 2)]

    def split(block):
        return (
            block[:, :width].reshape(experts * width, features),
            block[:, width:].reshape(experts * width, features),
        )

    x, y = split(inbound)
    out = 0.0
    dx = 0.0
    for (in_top, in_bottom), (out_top, out_bottom) in zip(ins, outs):
        wi = jnp.concatenate([in_top, in_bottom], axis=0)
        wo = jnp.concatenate([out_top, out_bottom], axis=0)
        act, slope = both(dot(x, wi, 1, 0))
        out = out + dot(act.astype(jnp.bfloat16), wo, 1, 0)
        grad = (dot(y, wo, 1, 1) * slope).astype(jnp.bfloat16)
        dx = dx + dot(grad, wi, 1, 1)
    back = jnp.concatenate(
        [
            out.astype(jnp.bfloat16).reshape(experts, width, features),
            dx.astype(jnp.bfloat16).reshape(experts, width, features),
        ],
        axis=1,
    )
    returned = lax.all_to_all(back, "expert", split_axis=0, concat_axis=0, tiled=True)
    grad_in = 0.0
    grad_out = 0.0
    for block in blocks:
        bx, by = split(block)
        act, slope = both(dot(bx, w_in, 1, 0))
        grad = (dot(by, w_out, 1, 1) * slope).astype(jnp.bfloat16)
        grad_out = grad_out + dot(act.astype(jnp.bfloat16), by, 0, 0)
        grad_in = grad_in + dot(bx, grad, 0, 0)
    final = dot(getting, returned.reshape(experts * 2 * width, features), 0, 0)
    layer_output = (final[:token_count] + final[token_count : 2 * token_count]).astype(jnp.bfloat16)
    input_grads = final[2 * token_count :].astype(jnp.bfloat16)
    return (
        layer_output,
        input_grads,
        grad_in.astype(jnp.bfloat16)[None],
        grad_out.astype(jnp.bfloat16)[None],
    )


def solution(mesh):
    return jax.shard_map(
        on_device,
        mesh=mesh,
        in_specs=(
            P(("expert", "dp"), None),
            P(("expert", "dp"), None),
            P(("expert", "dp"), None),
            P(("expert", "dp")),
            P(),
            P("expert", None, "dp"),
            P("expert", "dp", None),
            P(("expert", "dp"), None),
        ),
        out_specs=(
            P(("expert", "dp"), None),
            P(("expert", "dp"), None),
            P("expert", None, "dp"),
            P("expert", "dp", None),
        ),
        check_vma=False,
    )
```

```python
import jax
import jax.numpy as jnp
from jax import lax
from jax.experimental import pallas as pl
from jax.experimental.pallas import tpu as pltpu
from jax.sharding import PartitionSpec as P

F32 = jnp.float32
BF16 = jnp.bfloat16
VMEM_BYTES = 40 * 1024 * 1024


def moved(value, steps):
    count = lax.axis_size("dp")
    return lax.ppermute(value, "dp", [(s, (s + steps) % count) for s in range(count)])


def ring(one, two):
    left_one = moved(one, 1)
    right_two = moved(two, -1)
    left_two = moved(two, 1)
    right_one = moved(one, -1)
    far_one = moved(left_one, 1)
    far_two = moved(right_two, -1)
    return (left_one, left_two), (right_one, right_two), (far_one, far_two)


def dot(a, b, ca, cb):
    return lax.dot_general(a, b, (((ca,), (cb,)), ((), ())), preferred_element_type=F32)


def call(body, outs, flops, *args, smem=0):
    specs = [pl.BlockSpec(memory_space=pltpu.SMEM)] * smem
    specs += [pl.BlockSpec(memory_space=pltpu.VMEM)] * (len(args) - smem)
    shapes = [jax.ShapeDtypeStruct(s, d) for s, d in outs]
    moved_bytes = sum(a.size * a.dtype.itemsize for a in (*args, *shapes))
    return pl.pallas_call(
        body,
        out_shape=shapes,
        in_specs=specs,
        out_specs=[pl.BlockSpec(memory_space=pltpu.VMEM)] * len(outs),
        compiler_params=pltpu.CompilerParams(vmem_limit_bytes=VMEM_BYTES),
        cost_estimate=pl.CostEstimate(
            flops=flops, transcendentals=0, bytes_accessed=moved_bytes
        ),
    )(*args)


def prepare_body(capacity, spare):
    width = capacity + spare

    def body(count_ref, plan_ref, routes_ref, gates_ref, tok_ref, cot_ref, send_ref, get_ref):
        top_count, token_count = routes_ref.shape
        experts = send_ref.shape[0] // (2 * width)
        routes = routes_ref[...]
        gates = gates_ref[...].astype(F32)
        ids = lax.broadcasted_iota(jnp.int32, (experts, token_count), 0)
        times = lax.broadcasted_iota(jnp.int32, (experts, token_count), 1)
        hits = jnp.zeros((experts, token_count), F32)
        gate = jnp.zeros((experts, token_count), F32)
        for k in range(top_count):
            same = routes[k : k + 1, :] == ids
            hits = hits + jnp.where(same, 1.0, 0.0)
            gate = gate + jnp.where(same, gates[k : k + 1, :], 0.0)
        hits = jnp.where(times < count_ref[0], hits, 0.0)
        earlier = lax.broadcasted_iota(
            jnp.int32, (token_count, token_count), 0
        ) < lax.broadcasted_iota(jnp.int32, (token_count, token_count), 1)
        before = dot(hits.astype(BF16), jnp.where(earlier, 1.0, 0.0).astype(BF16), 1, 0)
        limit = jnp.full((experts, token_count), float(capacity), F32)
        hot = jnp.zeros((experts, token_count), F32)
        for i in range(plan_ref.shape[0]):
            hot = jnp.where(ids == plan_ref[i], 1.0, hot)
        limit = limit + float(spare) * hot
        place = jnp.where((hits > 0.0) & (before < limit), before, -1.0)
        rows = experts * 2 * width

        def spread(value):
            return jnp.broadcast_to(
                value[:, None, :], (experts, 2 * width, token_count)
            ).reshape(rows, token_count)

        row = lax.broadcasted_iota(jnp.int32, (rows, token_count), 0) % (2 * width)
        first = row < width
        slot = jnp.where(first, row, row - width).astype(F32)
        keep = spread(place) == slot
        one = jnp.where(keep, 1.0, 0.0)
        level = jnp.where(keep, spread(gate), 0.0)
        high = jnp.floor(level * (1.0 / 256.0))
        low = (level - 256.0 * high) * (1.0 / 65536.0)
        high = high * (1.0 / 256.0)
        zero = jnp.zeros_like(one)
        sending = jnp.concatenate(
            [
                jnp.where(first, one, zero).astype(BF16),
                jnp.where(first, zero, high).astype(BF16),
                jnp.where(first, zero, low).astype(BF16),
            ],
            axis=1,
        )
        source = jnp.concatenate([tok_ref[...], cot_ref[...], cot_ref[...]], axis=1)
        send_ref[...] = dot(sending, source, 1, 1).astype(BF16)
        get_ref[0:token_count, :] = jnp.where(first, high, zero).T.astype(BF16)
        get_ref[token_count : 2 * token_count, :] = jnp.where(first, low, zero).T.astype(BF16)
        get_ref[2 * token_count :, :] = jnp.where(first, zero, one).T.astype(BF16)

    return body


def place_matrix(rows, width, by_column):
    r = lax.broadcasted_iota(jnp.int32, (rows, rows), 1 if by_column else 0)
    q = lax.broadcasted_iota(jnp.int32, (rows, rows), 0 if by_column else 1)
    half = rows // 2
    second = r >= half
    inner = jnp.where(second, r - half, r)
    chunk = (inner // width) * (2 * width) + inner % width + jnp.where(second, width, 0)
    return jnp.where(q == chunk, 1.0, 0.0).astype(BF16)


def pack_body(width):
    def body(in_ref, x_ref, y_ref, xt_ref, yt_ref):
        rows = in_ref.shape[0]
        packed = dot(place_matrix(rows, width, False), in_ref[...], 1, 0).astype(BF16)
        x_ref[...] = packed[: rows // 2]
        y_ref[...] = packed[rows // 2 :]
        xt_ref[...] = packed[: rows // 2].T
        yt_ref[...] = packed[rows // 2 :].T

    return body


def hidden_terms(x, y, wi, wo):
    pre = dot(x, wi, 1, 0)
    s = jax.nn.sigmoid(1.702 * pre)
    act = (pre * s).astype(BF16)
    grad = dot(y, wo, 1, 1) * (s + 1.702 * pre * s * (1.0 - s))
    return act, grad.astype(BF16)


def near_body(x_ref, y_ref, *refs):
    out_ref, dx_ref = refs[-2:]
    weights = refs[:-2]
    x = x_ref[...]
    y = y_ref[...]
    for i in range(0, len(weights), 2):
        wi = weights[i][...]
        wo = weights[i + 1][...]
        act, grad = hidden_terms(x, y, wi, wo)
        if i == 0:
            out_ref[...] = dot(act, wo, 1, 0)
            dx_ref[...] = dot(grad, wi, 1, 1)
        else:
            out_ref[...] += dot(act, wo, 1, 0)
            dx_ref[...] += dot(grad, wi, 1, 1)


def far_body(width):
    def body(x_ref, y_ref, wi_ref, wo_ref, out_ref, dx_ref, back_ref):
        wi = wi_ref[...]
        wo = wo_ref[...]
        act, grad = hidden_terms(x_ref[...], y_ref[...], wi, wo)
        out = (out_ref[...] + dot(act, wo, 1, 0)).astype(BF16)
        dx = (dx_ref[...] + dot(grad, wi, 1, 1)).astype(BF16)
        rows = back_ref.shape[0]
        both = jnp.concatenate([out, dx], axis=0)
        back_ref[...] = dot(place_matrix(rows, width, True), both, 1, 0).astype(BF16)

    return body


def weight_terms(wi_t, wo, x, y):
    pre = dot(wi_t, x, 1, 0)
    s = jax.nn.sigmoid(1.702 * pre)
    act = (pre * s).astype(BF16)
    grad = (dot(wo, y, 1, 0) * (s + 1.702 * pre * s * (1.0 - s))).astype(BF16)
    return dot(grad, x, 1, 1), dot(act, y, 1, 1)


def near_weights_body(wi_ref, wo_ref, *refs):
    gi_ref, go_ref = refs[-2:]
    blocks = refs[:-2]
    wi_t = wi_ref[...]
    wo = wo_ref[...]
    for i in range(0, len(blocks), 2):
        term_in, term_out = weight_terms(wi_t, wo, blocks[i][...], blocks[i + 1][...])
        if i == 0:
            gi_ref[...] = term_in
            go_ref[...] = term_out
        else:
            gi_ref[...] += term_in
            go_ref[...] += term_out


def far_weights_body(wi_ref, wo_ref, x_ref, y_ref, si_ref, so_ref, gi_ref, go_ref):
    term_in, term_out = weight_terms(wi_ref[...], wo_ref[...], x_ref[...], y_ref[...])
    go_ref[...] = (so_ref[...] + term_out).astype(BF16)
    gi_ref[...] = (si_ref[...] + term_in).astype(BF16).T


def turn_body(in_ref, out_ref):
    out_ref[...] = in_ref[...].T


def finish_body(get_ref, back_ref, layer_ref, grads_ref):
    token_count = get_ref.shape[0] // 3
    final = dot(get_ref[...], back_ref[...], 1, 0)
    layer = final[:token_count] + final[token_count : 2 * token_count]
    layer_ref[...] = layer.T.astype(BF16)
    grads_ref[...] = final[2 * token_count :].T.astype(BF16)


def on_device(tokens, routes, gate_fixed, counts, replica_plan, weight_in, weight_out, cotangent):
    token_count, features = tokens.shape
    top_count = routes.shape[1]
    groups = lax.axis_size("expert")
    experts = groups * weight_in.shape[0]
    capacity = 3 * token_count * top_count // (8 * experts)
    spare = capacity // 2
    width = capacity + spare
    rows = experts * 2 * width
    half = rows // 2
    wi = weight_in[0]
    wo = weight_out[0]
    hidden = wo.shape[0]
    left_w, right_w, far_w = ring(wi, wo)
    send, get = call(
        prepare_body(capacity, spare),
        [((rows, features), BF16), ((3 * token_count, rows), BF16)],
        2 * rows * 3 * token_count * features,
        counts,
        replica_plan,
        routes.T,
        gate_fixed.T,
        tokens.T,
        cotangent.T,
        smem=2,
    )
    inbound = lax.all_to_all(
        send.reshape(experts, 2 * width, features), "expert", split_axis=0, concat_axis=0, tiled=True
    ).reshape(rows, features)
    product = 2 * half * features * hidden
    wi_late, left_w, right_w = lax.optimization_barrier((wi, left_w, right_w))
    (wi_t,) = call(turn_body, [((hidden, features), BF16)], 400 * product, wi_late)
    inbound, wi_t = lax.optimization_barrier((inbound, wi_t))
    x, y, xt, yt = call(
        pack_body(width),
        [((half, features), BF16)] * 2 + [((features, half), BF16)] * 2,
        2 * rows * rows * features,
        inbound,
    )
    out, dx = call(
        near_body,
        [((half, features), F32)] * 2,
        12 * product,
        x,
        y,
        wi,
        wo,
        *left_w,
        *right_w,
    )
    xt, yt, out = lax.optimization_barrier((xt, yt, out))
    left_r, right_r, far_r = ring(xt, yt)
    (back,) = call(
        far_body(width),
        [((rows, features), BF16)],
        4 * product + 2 * rows * rows * features,
        x,
        y,
        *far_w,
        out,
        dx,
    )
    returned = lax.all_to_all(
        back.reshape(experts, 2 * width, features), "expert", split_axis=0, concat_axis=0, tiled=True
    ).reshape(rows, features)
    sum_in, sum_out = call(
        near_weights_body,
        [((hidden, features), F32)] * 2,
        100 * product,
        wi_t,
        wo,
        xt,
        yt,
        *left_r,
        *right_r,
    )
    grad_in, grad_out = call(
        far_weights_body,
        [((features, hidden), BF16), ((hidden, features), BF16)],
        4 * product,
        wi_t,
        wo,
        *far_r,
        sum_in,
        sum_out,
    )
    layer, grads = call(
        finish_body,
        [((features, token_count), BF16)] * 2,
        2 * rows * 3 * token_count * features,
        get,
        returned,
    )
    return (layer.T, grads.T, grad_in[None], grad_out[None])


def solution(mesh):
    return jax.shard_map(
        on_device,
        mesh=mesh,
        in_specs=(
            P(("expert", "dp"), None),
            P(("expert", "dp"), None),
            P(("expert", "dp"), None),
            P(("expert", "dp")),
            P(),
            P("expert", None, "dp"),
            P("expert", "dp", None),
            P(("expert", "dp"), None),
        ),
        out_specs=(
            P(("expert", "dp"), None),
            P(("expert", "dp"), None),
            P("expert", None, "dp"),
            P("expert", "dp", None),
        ),
        check_vma=False,
    )
```

```python
import jax
import jax.numpy as jnp
from jax import lax
from jax.experimental import pallas as pl
from jax.experimental.pallas import tpu as pltpu
from jax.sharding import PartitionSpec as P

F32 = jnp.float32
BF16 = jnp.bfloat16
VMEM_BYTES = 32 * 1024 * 1024


def moved(value, steps):
    count = lax.axis_size("dp")
    return lax.ppermute(value, "dp", [(s, (s + steps) % count) for s in range(count)])


def ring(one, two):
    left_one = moved(one, 1)
    right_two = moved(two, -1)
    left_two = moved(two, 1)
    right_one = moved(one, -1)
    far_one = moved(left_one, 1)
    far_two = moved(right_two, -1)
    return (left_one, left_two), (right_one, right_two), (far_one, far_two)


def dot(a, b, ca, cb):
    return lax.dot_general(a, b, (((ca,), (cb,)), ((), ())), preferred_element_type=F32)


def call(body, outs, flops, *args, away=(), out_away=False, scratch=()):
    kinds = [
        pl.ANY if i in away else pltpu.SMEM if a.size == 1 else pltpu.VMEM
        for i, a in enumerate(args)
    ]
    specs = [pl.BlockSpec(memory_space=kind) for kind in kinds]
    args = [
        pltpu.with_memory_space_constraint(a, pltpu.HBM) if i in away else a
        for i, a in enumerate(args)
    ]
    shapes = [jax.ShapeDtypeStruct(s, d) for s, d in outs]
    moved_bytes = sum(a.size * a.dtype.itemsize for a in (*args, *shapes))
    return pl.pallas_call(
        body,
        out_shape=shapes,
        in_specs=specs,
        out_specs=[pl.BlockSpec(memory_space=pl.ANY if out_away else pltpu.VMEM)] * len(outs),
        scratch_shapes=list(scratch),
        compiler_params=pltpu.CompilerParams(vmem_limit_bytes=VMEM_BYTES),
        cost_estimate=pl.CostEstimate(
            flops=flops, transcendentals=0, bytes_accessed=moved_bytes
        ),
    )(*args)


def fetch(pairs, sems):
    copies = [pltpu.make_async_copy(src, dst, sems.at[i]) for i, (src, dst) in enumerate(pairs)]
    for copy in copies:
        copy.start()
    return copies


def table_scratch(plan_count, top_count, token_count):
    return [
        pltpu.SMEM((plan_count,), jnp.int32),
        pltpu.VMEM((top_count, token_count), jnp.int32),
        pltpu.VMEM((top_count, token_count), jnp.int32),
    ]


def tables(count_ref, plan_ref, routes_ref, gates_ref, experts, capacity, spare):
    width = capacity + spare
    top_count, token_count = routes_ref.shape
    routes = routes_ref[...]
    gates = gates_ref[...].astype(F32)
    ids = lax.broadcasted_iota(jnp.int32, (experts, token_count), 0)
    times = lax.broadcasted_iota(jnp.int32, (experts, token_count), 1)
    hits = jnp.zeros((experts, token_count), F32)
    gate = jnp.zeros((experts, token_count), F32)
    for k in range(top_count):
        same = routes[k : k + 1, :] == ids
        hits = hits + jnp.where(same, 1.0, 0.0)
        gate = gate + jnp.where(same, gates[k : k + 1, :], 0.0)
    hits = jnp.where(times < count_ref[0], hits, 0.0)
    earlier = lax.broadcasted_iota(
        jnp.int32, (token_count, token_count), 0
    ) < lax.broadcasted_iota(jnp.int32, (token_count, token_count), 1)
    before = dot(hits.astype(BF16), jnp.where(earlier, 1.0, 0.0).astype(BF16), 1, 0)
    hot = jnp.zeros((experts, token_count), F32)
    for i in range(plan_ref.shape[0]):
        hot = jnp.where(ids == plan_ref[i], 1.0, hot)
    limit = float(capacity) + float(spare) * hot
    place = jnp.where((hits > 0.0) & (before < limit), before, -1.0)
    rows = experts * 2 * width

    def spread(value):
        return jnp.broadcast_to(
            value[:, None, :], (experts, 2 * width, token_count)
        ).reshape(rows, token_count)

    row = lax.broadcasted_iota(jnp.int32, (rows, token_count), 0) % (2 * width)
    first = row < width
    slot = jnp.where(first, row, row - width).astype(F32)
    keep = spread(place) == slot
    one = jnp.where(keep, 1.0, 0.0)
    level = jnp.where(keep, spread(gate), 0.0)
    high = jnp.floor(level * (1.0 / 256.0))
    low = (level - 256.0 * high) * (1.0 / 65536.0)
    high = high * (1.0 / 256.0)
    return first, one, high, low


def prepare_body(capacity, spare):
    def body(
        count_ref,
        plan_hbm,
        routes_hbm,
        gates_hbm,
        tok_hbm,
        cot_hbm,
        send_ref,
        plan_ref,
        routes_ref,
        gates_ref,
        source_ref,
        sems,
    ):
        token_count = routes_ref.shape[1]
        experts = send_ref.shape[0] // (2 * (capacity + spare))
        copies = fetch(
            [
                (routes_hbm, routes_ref),
                (gates_hbm, gates_ref),
                (plan_hbm, plan_ref),
                (tok_hbm, source_ref.at[:, 0:token_count]),
                (cot_hbm, source_ref.at[:, token_count : 2 * token_count]),
                (cot_hbm, source_ref.at[:, 2 * token_count : 3 * token_count]),
            ],
            sems,
        )
        for copy in copies[:3]:
            copy.wait()
        first, one, high, low = tables(
            count_ref, plan_ref, routes_ref, gates_ref, experts, capacity, spare
        )
        zero = jnp.zeros_like(one)
        sending = jnp.concatenate(
            [
                jnp.where(first, one, zero).astype(BF16),
                jnp.where(first, zero, high).astype(BF16),
                jnp.where(first, zero, low).astype(BF16),
            ],
            axis=1,
        )
        for copy in copies[3:]:
            copy.wait()
        send_ref[...] = dot(sending, source_ref[...], 1, 1).astype(BF16)

    return body


def place_matrix(rows, width, by_column):
    r = lax.broadcasted_iota(jnp.int32, (rows, rows), 1 if by_column else 0)
    q = lax.broadcasted_iota(jnp.int32, (rows, rows), 0 if by_column else 1)
    half = rows // 2
    second = r >= half
    inner = jnp.where(second, r - half, r)
    chunk = (inner // width) * (2 * width) + inner % width + jnp.where(second, width, 0)
    return jnp.where(q == chunk, 1.0, 0.0).astype(BF16)


def hidden_terms(x, y, wi, wo):
    pre = dot(x, wi, 1, 0)
    s = jax.nn.sigmoid(1.702 * pre)
    act = (pre * s).astype(BF16)
    grad = dot(y, wo, 1, 1) * (s + 1.702 * pre * s * (1.0 - s))
    return act, grad.astype(BF16)


def near_body(width):
    def body(in_ref, *refs):
        weights = refs[:6]
        x_ref, y_ref, xt_ref, yt_ref, out_ref, dx_ref, wi_buf, wo_buf, sems = refs[6:]
        copies = fetch(
            [(w, (wo_buf if i % 2 else wi_buf).at[i // 2]) for i, w in enumerate(weights)], sems
        )
        place = place_matrix(in_ref.shape[0], width, False)
        packed = dot(place, in_ref[...], 1, 0).astype(BF16)
        half = x_ref.shape[0]
        x = packed[:half]
        y = packed[half:]
        x_ref[...] = x
        y_ref[...] = y
        xt_ref[...] = x.T
        yt_ref[...] = y.T
        for i in range(3):
            copies[2 * i].wait()
            copies[2 * i + 1].wait()
            wi = wi_buf[i]
            wo = wo_buf[i]
            act, grad = hidden_terms(x, y, wi, wo)
            if i == 0:
                out_ref[...] = dot(act, wo, 1, 0)
                dx_ref[...] = dot(grad, wi, 1, 1)
            else:
                out_ref[...] += dot(act, wo, 1, 0)
                dx_ref[...] += dot(grad, wi, 1, 1)

    return body


def far_body(width):
    def body(
        x_ref, y_ref, wi_hbm, wo_hbm, out_ref, dx_ref, back_hbm, wi_buf, wo_buf, back_buf, sems, back_sems
    ):
        copies = fetch([(wi_hbm, wi_buf), (wo_hbm, wo_buf)], sems)
        rows = back_buf.shape[0]
        spread = place_matrix(rows, width, True)
        copies[0].wait()
        wi = wi_buf[...]
        pre = dot(x_ref[...], wi, 1, 0)
        s = jax.nn.sigmoid(1.702 * pre)
        act = (pre * s).astype(BF16)
        copies[1].wait()
        wo = wo_buf[...]
        grad = (dot(y_ref[...], wo, 1, 1) * (s + 1.702 * pre * s * (1.0 - s))).astype(BF16)
        out = (out_ref[...] + dot(act, wo, 1, 0)).astype(BF16)
        dx = (dx_ref[...] + dot(grad, wi, 1, 1)).astype(BF16)
        both = jnp.concatenate([out, dx], axis=0)
        step = rows // 4
        leaving = []
        for i in range(4):
            lo = i * step
            back_buf[lo : lo + step, :] = dot(spread[lo : lo + step], both, 1, 0).astype(BF16)
            copy = pltpu.make_async_copy(
                back_buf.at[pl.ds(lo, step), :], back_hbm.at[pl.ds(lo, step), :], back_sems.at[i]
            )
            copy.start()
            leaving.append(copy)
        for copy in leaving:
            copy.wait()

    return body


def weight_terms(wi_t, wo, x, y):
    pre = dot(wi_t, x, 1, 0)
    s = jax.nn.sigmoid(1.702 * pre)
    act = (pre * s).astype(BF16)
    grad = (dot(wo, y, 1, 0) * (s + 1.702 * pre * s * (1.0 - s))).astype(BF16)
    return dot(grad, x, 1, 1), dot(act, y, 1, 1)


def near_weights_body(wi_ref, wo_ref, *refs):
    gi_ref, go_ref = refs[-2:]
    blocks = refs[:-2]
    wi_t = wi_ref[...]
    wo = wo_ref[...]
    for i in range(0, len(blocks), 2):
        term_in, term_out = weight_terms(wi_t, wo, blocks[i][...], blocks[i + 1][...])
        if i == 0:
            gi_ref[...] = term_in
            go_ref[...] = term_out
        else:
            gi_ref[...] += term_in
            go_ref[...] += term_out


def far_weights_body(wi_ref, wo_ref, x_ref, y_ref, si_ref, so_ref, gi_ref, go_ref):
    term_in, term_out = weight_terms(wi_ref[...], wo_ref[...], x_ref[...], y_ref[...])
    go_ref[...] = (so_ref[...] + term_out).astype(BF16)
    gi_ref[...] = (si_ref[...] + term_in).astype(BF16).T


def idle_body(capacity, spare):
    width = capacity + spare

    def body(
        count_ref,
        plan_hbm,
        routes_hbm,
        gates_hbm,
        in_ref,
        out_ref,
        get_ref,
        plan_ref,
        routes_ref,
        gates_ref,
        sems,
    ):
        copies = fetch(
            [
                (routes_hbm, routes_ref),
                (gates_hbm, gates_ref),
                (plan_hbm, plan_ref),
            ],
            sems,
        )
        out_ref[...] = in_ref[...].T
        for copy in copies:
            copy.wait()
        token_count = routes_ref.shape[1]
        first, one, high, low = tables(
            count_ref, plan_ref, routes_ref, gates_ref, get_ref.shape[1] // (2 * width), capacity, spare
        )
        zero = jnp.zeros_like(one)
        get_ref[0:token_count, :] = jnp.where(first, high, zero).T.astype(BF16)
        get_ref[token_count : 2 * token_count, :] = jnp.where(first, low, zero).T.astype(BF16)
        get_ref[2 * token_count :, :] = jnp.where(first, zero, one).T.astype(BF16)

    return body


def finish_body(get_ref, back_ref, layer_ref, grads_ref):
    token_count = get_ref.shape[0] // 3
    final = dot(get_ref[...], back_ref[...], 1, 0)
    layer = final[:token_count] + final[token_count : 2 * token_count]
    layer_ref[...] = layer.T.astype(BF16)
    grads_ref[...] = final[2 * token_count :].T.astype(BF16)


def on_device(tokens, routes, gate_fixed, counts, replica_plan, weight_in, weight_out, cotangent):
    token_count, features = tokens.shape
    top_count = routes.shape[1]
    groups = lax.axis_size("expert")
    experts = groups * weight_in.shape[0]
    capacity = 3 * token_count * top_count // (8 * experts)
    spare = capacity // 2
    width = capacity + spare
    rows = experts * 2 * width
    half = rows // 2
    wi = weight_in[0]
    wo = weight_out[0]
    hidden = wo.shape[0]
    left_w, right_w, far_w = ring(wi, wo)
    few = (counts, replica_plan, routes.T, gate_fixed.T)
    table = table_scratch(replica_plan.shape[0], top_count, token_count)
    (send,) = call(
        prepare_body(capacity, spare),
        [((rows, features), BF16)],
        2 * rows * 3 * token_count * features,
        *few,
        tokens.T,
        cotangent.T,
        away=range(1, 6),
        scratch=[
            *table,
            pltpu.VMEM((features, 3 * token_count), BF16),
            pltpu.SemaphoreType.DMA((6,)),
        ],
    )
    inbound = lax.all_to_all(
        send.reshape(experts, 2 * width, features), "expert", split_axis=0, concat_axis=0, tiled=True
    ).reshape(rows, features)
    product = 2 * half * features * hidden
    wi_late, left_one, right_two = lax.optimization_barrier((wi, left_w[0], right_w[1]))
    wi_t, get = call(
        idle_body(capacity, spare),
        [
            ((hidden, features), BF16),
            ((3 * token_count, rows), BF16),
        ],
        100 * product,
        *few,
        wi_late,
        away=range(1, 4),
        scratch=[*table, pltpu.SemaphoreType.DMA((3,))],
    )
    inbound, wi_t = lax.optimization_barrier((inbound, wi_t))
    left_w, right_w = (left_one, left_w[1]), (right_w[0], right_two)
    x, y, xt, yt, out, dx = call(
        near_body(width),
        [((half, features), BF16)] * 2
        + [((features, half), BF16)] * 2
        + [((half, features), F32)] * 2,
        12 * product + 2 * rows * rows * features,
        inbound,
        wi,
        wo,
        *left_w,
        *right_w,
        away=range(1, 7),
        scratch=[
            pltpu.VMEM((3, features, hidden), BF16),
            pltpu.VMEM((3, hidden, features), BF16),
            pltpu.SemaphoreType.DMA((6,)),
        ],
    )
    xt, yt, out = lax.optimization_barrier((xt, yt, out))
    left_r, right_r, far_r = ring(xt, yt)
    (back,) = call(
        far_body(width),
        [((rows, features), BF16)],
        4 * product + 2 * rows * rows * features,
        x,
        y,
        *far_w,
        out,
        dx,
        away=(2, 3),
        out_away=True,
        scratch=[
            pltpu.VMEM((features, hidden), BF16),
            pltpu.VMEM((hidden, features), BF16),
            pltpu.VMEM((rows, features), BF16),
            pltpu.SemaphoreType.DMA((2,)),
            pltpu.SemaphoreType.DMA((4,)),
        ],
    )
    returned = lax.all_to_all(
        back.reshape(experts, 2 * width, features), "expert", split_axis=0, concat_axis=0, tiled=True
    ).reshape(rows, features)
    sum_in, sum_out = call(
        near_weights_body,
        [((hidden, features), F32)] * 2,
        12 * product,
        wi_t,
        wo,
        xt,
        yt,
        *left_r,
        *right_r,
    )
    grad_in, grad_out = call(
        far_weights_body,
        [((features, hidden), BF16), ((hidden, features), BF16)],
        66 * product,
        wi_t,
        wo,
        *far_r,
        sum_in,
        sum_out,
    )
    layer, grads = call(
        finish_body,
        [((features, token_count), BF16)] * 2,
        2 * rows * 3 * token_count * features,
        get,
        returned,
    )
    return (layer.T, grads.T, grad_in[None], grad_out[None])


def solution(mesh):
    return jax.shard_map(
        on_device,
        mesh=mesh,
        in_specs=(
            P(("expert", "dp"), None),
            P(("expert", "dp"), None),
            P(("expert", "dp"), None),
            P(("expert", "dp")),
            P(),
            P("expert", None, "dp"),
            P("expert", "dp", None),
            P(("expert", "dp"), None),
        ),
        out_specs=(
            P(("expert", "dp"), None),
            P(("expert", "dp"), None),
            P("expert", None, "dp"),
            P("expert", "dp", None),
        ),
        check_vma=False,
    )
```

```python
import jax
import jax.numpy as jnp
from jax import lax
from jax.experimental import pallas as pl
from jax.experimental.pallas import tpu as pltpu
from jax.sharding import PartitionSpec as P

F32 = jnp.float32
BF16 = jnp.bfloat16
VMEM_BYTES = 32 * 1024 * 1024


def moved(value, steps):
    count = lax.axis_size("dp")
    return lax.ppermute(value, "dp", [(s, (s + steps) % count) for s in range(count)])


def ring(one, two):
    left_one = moved(one, 1)
    right_two = moved(two, -1)
    left_two = moved(two, 1)
    right_one = moved(one, -1)
    far_one = moved(left_one, 1)
    far_two = moved(right_two, -1)
    return (left_one, left_two), (right_one, right_two), (far_one, far_two)


def dot(a, b, ca, cb):
    return lax.dot_general(a, b, (((ca,), (cb,)), ((), ())), preferred_element_type=F32)


def call(body, outs, flops, *args, away=(), out_away=False, scratch=()):
    kinds = [
        pl.ANY if i in away else pltpu.SMEM if a.size == 1 else pltpu.VMEM
        for i, a in enumerate(args)
    ]
    specs = [pl.BlockSpec(memory_space=kind) for kind in kinds]
    args = [
        pltpu.with_memory_space_constraint(a, pltpu.HBM) if i in away else a
        for i, a in enumerate(args)
    ]
    shapes = [jax.ShapeDtypeStruct(s, d) for s, d in outs]
    moved_bytes = sum(a.size * a.dtype.itemsize for a in (*args, *shapes))
    return pl.pallas_call(
        body,
        out_shape=shapes,
        in_specs=specs,
        out_specs=[pl.BlockSpec(memory_space=pl.ANY if out_away else pltpu.VMEM)] * len(outs),
        scratch_shapes=list(scratch),
        compiler_params=pltpu.CompilerParams(vmem_limit_bytes=VMEM_BYTES),
        cost_estimate=pl.CostEstimate(
            flops=flops, transcendentals=0, bytes_accessed=moved_bytes
        ),
    )(*args)


def fetch(pairs, sems):
    copies = [pltpu.make_async_copy(src, dst, sems.at[i]) for i, (src, dst) in enumerate(pairs)]
    for copy in copies:
        copy.start()
    return copies


def table_scratch(plan_count, top_count, token_count):
    return [
        pltpu.SMEM((plan_count,), jnp.int32),
        pltpu.VMEM((top_count, token_count), jnp.int32),
        pltpu.VMEM((top_count, token_count), jnp.int32),
    ]


def tables(count_ref, plan_ref, routes_ref, gates_ref, experts, capacity, spare):
    width = capacity + spare
    top_count, token_count = routes_ref.shape
    routes = routes_ref[...]
    gates = gates_ref[...].astype(F32)
    ids = lax.broadcasted_iota(jnp.int32, (experts, token_count), 0)
    times = lax.broadcasted_iota(jnp.int32, (experts, token_count), 1)
    hits = jnp.zeros((experts, token_count), F32)
    gate = jnp.zeros((experts, token_count), F32)
    for k in range(top_count):
        same = routes[k : k + 1, :] == ids
        hits = hits + jnp.where(same, 1.0, 0.0)
        gate = gate + jnp.where(same, gates[k : k + 1, :], 0.0)
    hits = jnp.where(times < count_ref[0], hits, 0.0)
    earlier = lax.broadcasted_iota(
        jnp.int32, (token_count, token_count), 0
    ) < lax.broadcasted_iota(jnp.int32, (token_count, token_count), 1)
    before = dot(hits.astype(BF16), jnp.where(earlier, 1.0, 0.0).astype(BF16), 1, 0)
    hot = jnp.zeros((experts, token_count), F32)
    for i in range(plan_ref.shape[0]):
        hot = jnp.where(ids == plan_ref[i], 1.0, hot)
    limit = float(capacity) + float(spare) * hot
    place = jnp.where((hits > 0.0) & (before < limit), before, -1.0)
    rows = experts * 2 * width

    def spread(value):
        return jnp.broadcast_to(
            value[:, None, :], (experts, 2 * width, token_count)
        ).reshape(rows, token_count)

    row = lax.broadcasted_iota(jnp.int32, (rows, token_count), 0) % (2 * width)
    first = row < width
    slot = jnp.where(first, row, row - width).astype(F32)
    keep = spread(place) == slot
    one = jnp.where(keep, 1.0, 0.0)
    level = jnp.where(keep, spread(gate), 0.0)
    high = jnp.floor(level * (1.0 / 256.0))
    low = (level - 256.0 * high) * (1.0 / 65536.0)
    high = high * (1.0 / 256.0)
    return first, one, high, low


def prepare_body(capacity, spare):
    def body(
        count_ref,
        plan_hbm,
        routes_hbm,
        gates_hbm,
        tok_hbm,
        cot_hbm,
        send_ref,
        plan_ref,
        routes_ref,
        gates_ref,
        source_ref,
        sems,
    ):
        token_count = routes_ref.shape[1]
        experts = send_ref.shape[0] // (2 * (capacity + spare))
        copies = fetch(
            [
                (routes_hbm, routes_ref),
                (gates_hbm, gates_ref),
                (plan_hbm, plan_ref),
                (tok_hbm, source_ref.at[:, 0:token_count]),
                (cot_hbm, source_ref.at[:, token_count : 2 * token_count]),
                (cot_hbm, source_ref.at[:, 2 * token_count : 3 * token_count]),
            ],
            sems,
        )
        for copy in copies[:3]:
            copy.wait()
        first, one, high, low = tables(
            count_ref, plan_ref, routes_ref, gates_ref, experts, capacity, spare
        )
        zero = jnp.zeros_like(one)
        sending = jnp.concatenate(
            [
                jnp.where(first, one, zero).astype(BF16),
                jnp.where(first, zero, high).astype(BF16),
                jnp.where(first, zero, low).astype(BF16),
            ],
            axis=1,
        )
        for copy in copies[3:]:
            copy.wait()
        send_ref[...] = dot(sending, source_ref[...], 1, 1).astype(BF16)

    return body


def place_matrix(rows, width, by_column):
    r = lax.broadcasted_iota(jnp.int32, (rows, rows), 1 if by_column else 0)
    q = lax.broadcasted_iota(jnp.int32, (rows, rows), 0 if by_column else 1)
    half = rows // 2
    second = r >= half
    inner = jnp.where(second, r - half, r)
    chunk = (inner // width) * (2 * width) + inner % width + jnp.where(second, width, 0)
    return jnp.where(q == chunk, 1.0, 0.0).astype(BF16)


def hidden_terms(x, y, wi, wo):
    pre = dot(x, wi, 1, 0)
    s = jax.nn.sigmoid(1.702 * pre)
    act = (pre * s).astype(BF16)
    grad = dot(y, wo, 1, 1) * (s + 1.702 * pre * s * (1.0 - s))
    return act, grad.astype(BF16)


def near_body(width):
    def body(in_ref, *refs):
        weights = refs[:6]
        x_ref, y_ref, out_ref, dx_ref, wi_buf, wo_buf, sems = refs[6:]
        copies = fetch(
            [(w, (wo_buf if i % 2 else wi_buf).at[i // 2]) for i, w in enumerate(weights)], sems
        )
        place = place_matrix(in_ref.shape[0], width, False)
        packed = dot(place, in_ref[...], 1, 0).astype(BF16)
        half = x_ref.shape[0]
        x = packed[:half]
        y = packed[half:]
        x_ref[...] = x
        y_ref[...] = y
        for i in range(3):
            copies[2 * i].wait()
            copies[2 * i + 1].wait()
            wi = wi_buf[i]
            wo = wo_buf[i]
            act, grad = hidden_terms(x, y, wi, wo)
            if i == 0:
                out_ref[...] = dot(act, wo, 1, 0)
                dx_ref[...] = dot(grad, wi, 1, 1)
            else:
                out_ref[...] += dot(act, wo, 1, 0)
                dx_ref[...] += dot(grad, wi, 1, 1)

    return body


def far_body(width):
    def body(
        x_ref, y_ref, wi_hbm, wo_hbm, out_ref, dx_ref, back_hbm, wi_buf, wo_buf, back_buf, sems, back_sems
    ):
        copies = fetch([(wi_hbm, wi_buf), (wo_hbm, wo_buf)], sems)
        rows = back_buf.shape[0]
        spread = place_matrix(rows, width, True)
        copies[0].wait()
        wi = wi_buf[...]
        pre = dot(x_ref[...], wi, 1, 0)
        s = jax.nn.sigmoid(1.702 * pre)
        act = (pre * s).astype(BF16)
        copies[1].wait()
        wo = wo_buf[...]
        grad = (dot(y_ref[...], wo, 1, 1) * (s + 1.702 * pre * s * (1.0 - s))).astype(BF16)
        out = (out_ref[...] + dot(act, wo, 1, 0)).astype(BF16)
        dx = (dx_ref[...] + dot(grad, wi, 1, 1)).astype(BF16)
        both = jnp.concatenate([out, dx], axis=0)
        step = rows // 4
        leaving = []
        for i in range(4):
            lo = i * step
            back_buf[lo : lo + step, :] = dot(spread[lo : lo + step], both, 1, 0).astype(BF16)
            copy = pltpu.make_async_copy(
                back_buf.at[pl.ds(lo, step), :], back_hbm.at[pl.ds(lo, step), :], back_sems.at[i]
            )
            copy.start()
            leaving.append(copy)
        for copy in leaving:
            copy.wait()

    return body


def weight_terms(wi_t, wo, x, y):
    pre = dot(wi_t, x, 1, 0)
    s = jax.nn.sigmoid(1.702 * pre)
    act = (pre * s).astype(BF16)
    grad = (dot(wo, y, 1, 0) * (s + 1.702 * pre * s * (1.0 - s))).astype(BF16)
    return dot(grad, x, 1, 1), dot(act, y, 1, 1)


def turn_body(x_ref, y_ref, both_ref):
    half = x_ref.shape[0]
    both_ref[:, :half] = x_ref[...].T
    both_ref[:, half:] = y_ref[...].T


def near_weights_body(wi_ref, wo_ref, *refs):
    gi_ref, go_ref = refs[-2:]
    wi_t = wi_ref[...]
    wo = wo_ref[...]
    for i, both_ref in enumerate(refs[:-2]):
        half = both_ref.shape[1] // 2
        term_in, term_out = weight_terms(wi_t, wo, both_ref[:, :half], both_ref[:, half:])
        if i == 0:
            gi_ref[...] = term_in
            go_ref[...] = term_out
        else:
            gi_ref[...] += term_in
            go_ref[...] += term_out


def far_weights_body(wi_ref, wo_ref, x_ref, y_ref, si_ref, so_ref, gi_ref, go_ref):
    term_in, term_out = weight_terms(wi_ref[...], wo_ref[...], x_ref[...], y_ref[...])
    go_ref[...] = (so_ref[...] + term_out).astype(BF16)
    gi_ref[...] = (si_ref[...] + term_in).astype(BF16).T


def idle_body(capacity, spare):
    width = capacity + spare

    def body(
        count_ref,
        plan_hbm,
        routes_hbm,
        gates_hbm,
        in_ref,
        out_ref,
        get_ref,
        plan_ref,
        routes_ref,
        gates_ref,
        sems,
    ):
        copies = fetch(
            [
                (routes_hbm, routes_ref),
                (gates_hbm, gates_ref),
                (plan_hbm, plan_ref),
            ],
            sems,
        )
        out_ref[...] = in_ref[...].T
        for copy in copies:
            copy.wait()
        token_count = routes_ref.shape[1]
        first, one, high, low = tables(
            count_ref, plan_ref, routes_ref, gates_ref, get_ref.shape[1] // (2 * width), capacity, spare
        )
        zero = jnp.zeros_like(one)
        get_ref[0:token_count, :] = jnp.where(first, high, zero).T.astype(BF16)
        get_ref[token_count : 2 * token_count, :] = jnp.where(first, low, zero).T.astype(BF16)
        get_ref[2 * token_count :, :] = jnp.where(first, zero, one).T.astype(BF16)

    return body


def finish_body(get_ref, back_ref, layer_ref, grads_ref):
    token_count = get_ref.shape[0] // 3
    final = dot(get_ref[...], back_ref[...], 1, 0)
    layer = final[:token_count] + final[token_count : 2 * token_count]
    layer_ref[...] = layer.T.astype(BF16)
    grads_ref[...] = final[2 * token_count :].T.astype(BF16)


def on_device(tokens, routes, gate_fixed, counts, replica_plan, weight_in, weight_out, cotangent):
    token_count, features = tokens.shape
    top_count = routes.shape[1]
    groups = lax.axis_size("expert")
    experts = groups * weight_in.shape[0]
    capacity = 3 * token_count * top_count // (8 * experts)
    spare = capacity // 2
    width = capacity + spare
    rows = experts * 2 * width
    half = rows // 2
    wi = weight_in[0]
    wo = weight_out[0]
    hidden = wo.shape[0]
    left_w, right_w, far_w = ring(wi, wo)
    few = (counts, replica_plan, routes.T, gate_fixed.T)
    table = table_scratch(replica_plan.shape[0], top_count, token_count)
    (send,) = call(
        prepare_body(capacity, spare),
        [((rows, features), BF16)],
        2 * rows * 3 * token_count * features,
        *few,
        tokens.T,
        cotangent.T,
        away=range(1, 6),
        scratch=[
            *table,
            pltpu.VMEM((features, 3 * token_count), BF16),
            pltpu.SemaphoreType.DMA((6,)),
        ],
    )
    inbound = lax.all_to_all(
        send.reshape(experts, 2 * width, features), "expert", split_axis=0, concat_axis=0, tiled=True
    ).reshape(rows, features)
    product = 2 * half * features * hidden
    wi_late, left_one, right_two = lax.optimization_barrier((wi, left_w[0], right_w[1]))
    wi_t, get = call(
        idle_body(capacity, spare),
        [
            ((hidden, features), BF16),
            ((3 * token_count, rows), BF16),
        ],
        100 * product,
        *few,
        wi_late,
        away=range(1, 4),
        scratch=[*table, pltpu.SemaphoreType.DMA((3,))],
    )
    inbound, wi_t = lax.optimization_barrier((inbound, wi_t))
    left_w, right_w = (left_one, left_w[1]), (right_w[0], right_two)
    x, y, out, dx = call(
        near_body(width),
        [((half, features), BF16)] * 2
        + [((half, features), F32)] * 2,
        12 * product + 2 * rows * rows * features,
        inbound,
        wi,
        wo,
        *left_w,
        *right_w,
        away=range(1, 7),
        scratch=[
            pltpu.VMEM((3, features, hidden), BF16),
            pltpu.VMEM((3, hidden, features), BF16),
            pltpu.SemaphoreType.DMA((6,)),
        ],
    )
    (both,) = call(turn_body, [((features, rows), BF16)], 0, x, y)
    left_r = moved(both, 1)
    right_r = moved(both, -1)
    far_r = (moved(left_r[:, :half], 1), moved(right_r[:, half:], -1))
    (back,) = call(
        far_body(width),
        [((rows, features), BF16)],
        4 * product + 2 * rows * rows * features,
        x,
        y,
        *far_w,
        out,
        dx,
        away=(2, 3),
        out_away=True,
        scratch=[
            pltpu.VMEM((features, hidden), BF16),
            pltpu.VMEM((hidden, features), BF16),
            pltpu.VMEM((rows, features), BF16),
            pltpu.SemaphoreType.DMA((2,)),
            pltpu.SemaphoreType.DMA((4,)),
        ],
    )
    returned = lax.all_to_all(
        back.reshape(experts, 2 * width, features), "expert", split_axis=0, concat_axis=0, tiled=True
    ).reshape(rows, features)
    sum_in, sum_out = call(
        near_weights_body,
        [((hidden, features), F32)] * 2,
        8 * product,
        wi_t,
        wo,
        both,
        left_r,
        right_r,
    )
    grad_in, grad_out = call(
        far_weights_body,
        [((features, hidden), BF16), ((hidden, features), BF16)],
        50 * product,
        wi_t,
        wo,
        *far_r,
        sum_in,
        sum_out,
    )
    layer, grads = call(
        finish_body,
        [((features, token_count), BF16)] * 2,
        2 * rows * 3 * token_count * features,
        get,
        returned,
    )
    return (layer.T, grads.T, grad_in[None], grad_out[None])


def solution(mesh):
    return jax.shard_map(
        on_device,
        mesh=mesh,
        in_specs=(
            P(("expert", "dp"), None),
            P(("expert", "dp"), None),
            P(("expert", "dp"), None),
            P(("expert", "dp")),
            P(),
            P("expert", None, "dp"),
            P("expert", "dp", None),
            P(("expert", "dp"), None),
        ),
        out_specs=(
            P(("expert", "dp"), None),
            P(("expert", "dp"), None),
            P("expert", None, "dp"),
            P("expert", "dp", None),
        ),
        check_vma=False,
    )
```
